512 devices in a mesh: energy: 64 (over y_hi, x, z), slab: 8 (over y_lo, core).
Axes of the slice: x: 4, y: 8 (y_hi: 2, y_lo: 4; y = y_hi * 4 + y_lo), z: 8, core: 2. Of those that a mesh axis runs over, the one named last changes fastest.
Arguments:
- green_local: bfloat16 [128, 8, 2, 512, 512], P('energy', 'slab'), may hold values from -2.5 to 2.5
- coupling: bfloat16 [8, 512, 512], P('slab', 'energy'), may hold values from -0.21875 to 0.21875
- masks: int32 [8, 4, 4], P('slab'), may hold values 0 or 1
- incident: bfloat16 [128, 8, 512, 2, 128], P('energy', 'slab'), may hold values from -3 to 3
- energy_index: int32 [128], P('energy'), may hold values from 0 to 255
Outputs:
- wave_field: bfloat16 [128, 8, 512, 2, 128], P('energy', 'slab')
- outflow: bfloat16 [128, 8, 512, 2, 128], P('energy', 'slab')
- density: float32 [8, 512, 2, 512], P('slab', 'energy')
The draws below stay inside these ranges and needn't reach their ends.
All inputs are finite; a program needn't handle non-finite values. No bound on the sum of `masks` on one device may be relied on, other than what follows from the above.
Results may differ from the reference program's by a relative error of at most 0.027.
Values may be sent and summed in bfloat16 or wider, within the bound.
No kernel may reach another device: no remote copies, remote signals or barrier semaphores. Data moves between devices by JAX's collectives and lax.ppermute only.
A program may use at most 64 MiB of HBM per device.

```python
import math
import jax
import jax.numpy as jnp
from jax import lax

M = 512
BLK = 128
MB = 4
MODES = 128
ENERGIES = 128
SLABS = 8


def draw_green_local(key, part):
    noise_key = jax.random.fold_in(key, 11)
    size_key = jax.random.fold_in(key, 12)
    angle_key = jax.random.fold_in(key, 13)
    full_shape = (ENERGIES, SLABS, 2, M, M)
    row_shape = (ENERGIES, SLABS, 1, M, 1)
    noise = jnp.clip(jax.random.normal(noise_key, full_shape, jnp.float32), -4.0, 4.0) * (0.5 / math.sqrt(M))
    amplitude = jnp.exp(jax.random.uniform(size_key, row_shape, jnp.float32, math.log(0.6), math.log(1.4)))
    angles = jax.random.uniform(angle_key, row_shape, jnp.float32, -math.pi, 0.0)
    diagonal = jnp.concatenate([jnp.cos(angles), jnp.sin(angles)], axis=2) * amplitude
    identity_matrix = jnp.eye(M, dtype=jnp.float32)
    result = noise + diagonal * identity_matrix
    return result.astype(jnp.bfloat16)


def plant(values, own_key, least, top_value):
    spot = [jax.random.randint(jax.random.fold_in(own_key, axis), (), 0, length) for axis, length in enumerate(values.shape)]
    longest = values.shape.index(max(values.shape))
    neighbour = spot[:longest] + [(spot[longest] + 1) % values.shape[longest]] + spot[longest + 1:]
    return values.at[tuple(spot)].set(least).at[tuple(neighbour)].set(top_value)


def block_scale(rng, extent, split, smallest, top_value):
    def one(dim, shards_of):
        steps = jax.random.uniform(jax.random.fold_in(jax.random.fold_in(rng, 6), dim), (shards_of,), jnp.float32, smallest / len(split), top_value / len(split))
        return jnp.repeat(jnp.exp(steps), extent[dim] // shards_of).reshape((-1,) + (1,) * (len(extent) - dim - 1))

    gain = one(*split[0])
    for cut in split[1:]:
        gain = gain * one(*cut)
    return gain


def normal_values(stream_key, extent, deviation, limit, cuts=(), kind=jnp.bfloat16):
    drawn = deviation * jax.random.normal(stream_key, extent, jnp.float32)
    if cuts:
        drawn = drawn * block_scale(stream_key, extent, cuts, -0.22, 0.18)
    return jnp.clip(drawn, -limit, limit).astype(kind)


def setup_inputs(seed: int = 0) -> dict:
    splits = jax.random.split(jax.random.key(seed), 6)
    green_local = draw_green_local(jax.random.fold_in(splits[5], 71), 0)
    coupling = normal_values(splits[1], (SLABS, M, M), (3 * M // 2) ** -0.5, 0.21875, ((0, 8), (1, 64)))
    masks = plant((jax.random.randint(splits[2], (SLABS, MB, MB), 0, 4) < 3).astype(jnp.int32), jax.random.fold_in(splits[2], 1), 0, 1)
    incident = normal_values(splits[3], (ENERGIES, SLABS, M, 2, MODES), 0.5, 3.0, ((0, 64), (1, 8)))
    energy_index = plant(jax.random.randint(splits[4], (ENERGIES,), 0, 256), jax.random.fold_in(splits[4], 1), 0, 255).astype(jnp.int32)
    return {"green_local": green_local, "coupling": coupling, "masks": masks, "incident": incident, "energy_index": energy_index}


def apply_green(green_block, vector):
    orbitals = green_block.shape[1]
    mode_count = vector.shape[2]
    product = jnp.dot(green_block.reshape(2 * orbitals, orbitals), vector.reshape(orbitals, 2 * mode_count), preferred_element_type=jnp.float32)
    product = product.reshape(2, orbitals, 2, mode_count)
    real_part = product[0, :, 0] - product[1, :, 1]
    imag_part = product[0, :, 1] + product[1, :, 0]
    return jnp.stack([real_part, imag_part], axis=1).astype(jnp.bfloat16)


def couple_forward(matrix, vector):
    orbitals = vector.shape[0]
    product = jnp.dot(matrix, vector.reshape(orbitals, -1), preferred_element_type=jnp.float32)
    return product.reshape(vector.shape)


def couple_back(matrix, vector):
    orbitals = vector.shape[0]
    product = lax.dot_general(matrix, vector.reshape(orbitals, -1), (((0,), (0,)), ((), ())), preferred_element_type=jnp.float32)
    return product.reshape(vector.shape)


def relax(green_block, source_here, left_term, matrix, right_wave):
    summed = source_here.astype(jnp.float32) + left_term.astype(jnp.float32) + couple_forward(matrix, right_wave)
    return apply_green(green_block, summed.astype(jnp.bfloat16))


def fermi(index_values, scale):
    exponent = (index_values.astype(jnp.float32) - 128.0) / 24.0
    return scale / (1.0 + jnp.exp(exponent))


def reference(green_local, coupling, masks, incident, energy_index):
    opened = jnp.repeat(jnp.repeat(masks, BLK, axis=1), BLK, axis=2)
    coupled = coupling * opened.astype(jnp.bfloat16)

    def one_energy(energy_item):
        green_here, source = energy_item
        first_waves = [apply_green(green_here[slab_index], source[slab_index]) for slab_index in range(SLABS)]
        zero_wave = jnp.zeros_like(first_waves[0])
        incoming = zero_wave
        left_terms = []
        for slab_index in range(SLABS):
            right_wave = first_waves[slab_index + 1] if slab_index + 1 < SLABS else zero_wave
            relaxed = relax(green_here[slab_index], source[slab_index], incoming, coupled[slab_index], right_wave)
            left_terms.append(incoming)
            incoming = couple_back(coupled[slab_index], relaxed).astype(jnp.bfloat16)
        final_waves = [zero_wave] * SLABS
        after = zero_wave
        for slab_index in reversed(range(SLABS)):
            after = relax(green_here[slab_index], source[slab_index], left_terms[slab_index], coupled[slab_index], after)
            final_waves[slab_index] = after
        outflow_list = [couple_back(coupled[slab_index], final_waves[slab_index]).astype(jnp.bfloat16) for slab_index in range(SLABS)]
        return jnp.stack(final_waves), jnp.stack(outflow_list)

    wave_field, outflow = lax.map(one_energy, (green_local, incident))
    weights = fermi(energy_index, 4.0 / (ENERGIES * MODES))

    def slab_density(slab_waves):
        scaled = (slab_waves.astype(jnp.float32) * weights[:, None, None, None]).astype(jnp.bfloat16)
        left_side = scaled.transpose(1, 0, 2, 3).reshape(M, -1)
        right_real = slab_waves.transpose(1, 0, 2, 3).reshape(M, -1)
        right_imag = jnp.stack([-slab_waves[:, :, 1], slab_waves[:, :, 0]], axis=2).transpose(1, 0, 2, 3).reshape(M, -1)
        real_part = lax.dot_general(left_side, right_real, (((1,), (1,)), ((), ())), preferred_element_type=jnp.float32)
        imag_part = lax.dot_general(left_side, right_imag, (((1,), (1,)), ((), ())), preferred_element_type=jnp.float32)
        return jnp.stack([real_part, imag_part], axis=1)

    density = lax.map(slab_density, wave_field.transpose(1, 0, 2, 3, 4))
    return (wave_field, outflow, density)
```

```python
import jax
import jax.numpy as jnp
from jax import lax
from jax.sharding import PartitionSpec as P

BF16 = jnp.bfloat16
F32 = jnp.float32


def chip_hop(block, distance):
    size = lax.axis_size("slab")
    route = [(i, i + 2 * distance) for i in range(size) if 0 <= i + 2 * distance < size]
    return lax.ppermute(block, "slab", route)


def chip_swap(block):
    size = lax.axis_size("slab")
    pairs = [[i, i + 1] for i in range(0, size, 2)]
    return lax.all_to_all(block, "slab", 0, 0, axis_index_groups=pairs, tiled=True)


def mul(left, right, dims=((1,), (0,))):
    return lax.dot_general(left, right, (dims, ((), ())), preferred_element_type=F32)


def complex_apply(matrix, vector):
    n = matrix.shape[1]
    k = vector.shape[1] // 2
    product = mul(matrix.reshape(2 * n, -1), vector)
    real = product[:n, :k] - product[n:, k:]
    imag = product[:n, k:] + product[n:, :k]
    return jnp.concatenate([real, imag], axis=1)


def complex_product(left, right):
    n = left.shape[1]
    stacked = left.reshape(2 * n, -1)
    pr = mul(stacked, right[0])
    pi = mul(stacked, right[1])
    return jnp.stack([pr[:n] - pi[n:], pi[:n] + pr[n:]]).astype(BF16)


def transposed_times(coupled, matrix):
    return jnp.stack([mul(coupled, matrix[0], ((0,), (0,))), mul(coupled, matrix[1], ((0,), (0,)))]).astype(BF16)


def times(matrix, coupled):
    n = matrix.shape[1]
    return mul(matrix.reshape(2 * n, n), coupled).reshape(2, n, n).astype(BF16)


def fermi(index_values, scale):
    exponent = (index_values.astype(F32) - 128.0) / 24.0
    return scale / (1.0 + jnp.exp(exponent))


def shards(green_local, coupling, masks, incident, energy_index):
    count = green_local.shape[0]
    n = green_local.shape[3]
    modes = incident.shape[4]
    devices = lax.axis_size("energy")
    rows = coupling.shape[1]
    tile = n // masks.shape[1]

    by_row = jnp.repeat(masks[0].astype(BF16), tile, axis=0)
    here = lax.dynamic_slice_in_dim(by_row, lax.axis_index("energy") * rows, rows, 0)
    mine = coupling[0] * jnp.repeat(here, tile, axis=1)
    whole = lax.all_to_all(jnp.tile(mine, (devices, 1)), "energy", 0, 0, tiled=True)

    green = chip_swap(green_local[:, 0])
    source = chip_swap(incident[:, 0].reshape(count, n, 2 * modes))
    green_a, green_b = green[0], green[1]
    source_a, source_b = source[0], source[1]
    first_a = complex_apply(green_a, source_a).astype(BF16)
    first_b = complex_apply(green_b, source_b).astype(BF16)
    first_next = chip_hop(first_a, -1)

    size = lax.axis_size("slab")
    pairs = [[i, i + 1] for i in range(0, size, 2)]
    both = lax.all_gather(whole, "slab", axis=0, axis_index_groups=pairs)
    c_a, c_b = both[0], both[1]

    base_a = source_a.astype(F32) + mul(c_a, first_b)
    base_b = source_b.astype(F32) + mul(c_b, first_next)
    step_a = transposed_times(c_a, green_a)
    step_b = transposed_times(c_b, green_b)
    passed = complex_apply(step_a, base_a.astype(BF16))
    start = complex_apply(step_b, (base_b + passed).astype(BF16))
    flux = chip_hop(start.astype(BF16), 1)
    through = complex_product(step_b, step_a)
    for _ in range(size // 2 - 2):
        flux = chip_hop((start + complex_apply(through, flux)).astype(BF16), 1)

    flux_a = complex_apply(step_a, (base_a + flux.astype(F32)).astype(BF16)).astype(BF16)
    left_a = source_a.astype(F32) + flux.astype(F32)
    left_b = source_b.astype(F32) + flux_a.astype(F32)
    back_a = times(green_a, c_a)
    back_b = times(green_b, c_b)
    back = complex_product(back_a, back_b)
    wave_b = complex_apply(green_b, left_b.astype(BF16)).astype(BF16)
    start = complex_apply(green_a, (left_a + mul(c_a, wave_b)).astype(BF16))
    wave_in = chip_hop(start.astype(BF16), -1)
    for _ in range(size // 2 - 2):
        wave_in = chip_hop((start + complex_apply(back, wave_in)).astype(BF16), -1)
    wave_b = complex_apply(green_b, (left_b + mul(c_b, wave_in)).astype(BF16)).astype(BF16)
    wave_a = complex_apply(green_a, (left_a + mul(c_a, wave_b)).astype(BF16)).astype(BF16)

    wave = chip_swap(jnp.stack([wave_a, wave_b]))
    weights = fermi(energy_index, 4.0 / (count * devices * modes))
    scaled = (wave.astype(F32) * weights[:, None, None]).astype(BF16)
    real = sum(mul(scaled[e], wave[e], ((1,), (1,))) for e in range(count))
    turned = jnp.concatenate([-wave[:, :, modes:], wave[:, :, :modes]], axis=2)
    imag = sum(mul(scaled[e], turned[e], ((1,), (1,))) for e in range(count))
    partial = jnp.concatenate([real, imag], axis=1).astype(BF16)
    parts = lax.all_to_all(partial, "energy", 0, 0, tiled=True).reshape(devices, n // devices, 2 * n)
    density = jnp.sum(parts.astype(F32), axis=0).reshape(1, n // devices, 2, n)

    own = whole
    outflow = jnp.stack([mul(own, wave[e], ((0,), (0,))) for e in range(count)]).astype(BF16)
    shape = (count, 1, n, 2, modes)
    return (wave.reshape(shape), outflow.reshape(shape), density)


def solution(mesh):
    return jax.shard_map(
        shards,
        mesh=mesh,
        in_specs=(
            P("energy", "slab", None, None, None),
            P("slab", "energy", None),
            P("slab", None, None),
            P("energy", "slab", None, None, None),
            P("energy"),
        ),
        out_specs=(
            P("energy", "slab", None, None, None),
            P("energy", "slab", None, None, None),
            P("slab", "energy", None, None),
        ),
        check_vma=False,
    )
```

```python
import jax
import jax.numpy as jnp
from jax import lax
from jax.experimental import pallas as pl
from jax.experimental.pallas import tpu as pltpu
from jax.sharding import PartitionSpec as P

BF16 = jnp.bfloat16
F32 = jnp.float32


def chip_hop(block, distance):
    size = lax.axis_size("slab")
    route = [(i, i + 2 * distance) for i in range(size) if 0 <= i + 2 * distance < size]
    return lax.ppermute(block, "slab", route)


def swap(block):
    route = [(i, i ^ 1) for i in range(lax.axis_size("slab"))]
    return lax.ppermute(block, "slab", route)


def pick(blocks, index):
    return lax.dynamic_index_in_dim(blocks, index, 0, keepdims=False)


def ordered(core, kept, got):
    even = core == 0
    return jnp.stack([jnp.where(even, kept, got), jnp.where(even, got, kept)])


def exchange(block, groups):
    return lax.all_to_all(block, "energy", 0, 0, axis_index_groups=groups, tiled=True)


def energy_grid(devices):
    return (2, 2, 2) if devices == 8 else (2, 4, devices // 8)


def mul(left, right):
    return lax.dot_general(left, right, (((1,), (0,)), ((), ())), preferred_element_type=F32)


def mul_transposed(left, right):
    return lax.dot_general(left, right, (((1,), (1,)), ((), ())), preferred_element_type=F32)


def turned(vector):
    k = vector.shape[1] // 2
    return jnp.concatenate([-vector[:, k:], vector[:, :k]], axis=1)


def apply(real, imag, vector):
    return mul(real, vector) + mul(imag, turned(vector))


def product(left, right, out):
    lr, li, rr, ri = left[0], left[1], right[0], right[1]
    out[0] = (mul(lr, rr) - mul(li, ri)).astype(BF16)
    out[1] = (mul(lr, ri) + mul(li, rr)).astype(BF16)


def begin_kernel(g, c, ct, src, first, following, base, start, send):
    base_a = src[0].astype(F32) + mul(c[0], first[1])
    base[...] = base_a
    field = apply(g[0, 0], g[0, 1], base_a.astype(BF16)).astype(BF16)
    summed = src[1].astype(F32) + mul(c[1], following[...]) + mul(ct[0], field)
    field = apply(g[1, 0], g[1, 1], summed.astype(BF16)).astype(BF16)
    flux = mul(ct[1], field)
    start[...] = flux
    send[...] = flux.astype(BF16)


def compose_kernel(g, ct, step_a, through, step_b):
    step_a[0] = mul(ct[0], g[0, 0]).astype(BF16)
    step_a[1] = mul(ct[0], g[0, 1]).astype(BF16)
    step_b[0] = mul(ct[1], g[1, 0]).astype(BF16)
    step_b[1] = mul(ct[1], g[1, 1]).astype(BF16)
    product(step_b, step_a, through)


def compose_back_kernel(g, c, back, back_a, back_b):
    back_a[0] = mul(g[0, 0], c[0]).astype(BF16)
    back_a[1] = mul(g[0, 1], c[0]).astype(BF16)
    back_b[0] = mul(g[1, 0], c[1]).astype(BF16)
    back_b[1] = mul(g[1, 1], c[1]).astype(BF16)
    product(back_a, back_b, back)


def hop_kernel(matrix, start, arrived, send):
    send[...] = (start[...] + apply(matrix[0], matrix[1], arrived[...])).astype(BF16)


def turn_kernel(g, c, step_a, src, base, flux, left, start, send):
    arrived = flux[...].astype(F32)
    summed = (base[...] + arrived).astype(BF16)
    flux_a = apply(step_a[0], step_a[1], summed)
    left_a = src[0].astype(F32) + arrived
    left_b = src[1].astype(F32) + flux_a
    left[0] = left_a
    left[1] = left_b
    field = apply(g[1, 0], g[1, 1], left_b.astype(BF16)).astype(BF16)
    summed = (left_a + mul(c[0], field)).astype(BF16)
    wave = apply(g[0, 0], g[0, 1], summed)
    start[...] = wave
    send[...] = wave.astype(BF16)


def finish_kernel(core, g, c, left, arrived, keep, send):
    summed = (left[1] + mul(c[1], arrived[...])).astype(BF16)
    wave_b = apply(g[1, 0], g[1, 1], summed).astype(BF16)
    summed = (left[0] + mul(c[0], wave_b)).astype(BF16)
    wave_a = apply(g[0, 0], g[0, 1], summed).astype(BF16)

    @pl.when(core[0] == 0)
    def _():
        keep[...] = wave_a
        send[...] = wave_b

    @pl.when(core[0] != 0)
    def _():
        keep[...] = wave_b
        send[...] = wave_a


def density_kernel(core, weights, kept, got, out):
    n, _ = kept.shape
    outer, inner, rows, _ = out.shape
    here = weights[core[0]]
    there = weights[1 - core[0]]
    real = jnp.zeros((n, n), F32)
    imag = jnp.zeros((n, n), F32)
    for weight, wave in ((here, kept), (there, got)):
        w = wave[...]
        scaled = (w.astype(F32) * weight).astype(BF16)
        real = real + mul_transposed(scaled, w)
        imag = imag + mul_transposed(scaled, turned(w))
    real = real.astype(BF16)
    imag = imag.astype(BF16)
    for i in range(outer):
        for j in range(inner):
            first = (j * outer + i) * rows
            out[i, j, :, :n] = real[first : first + rows]
            out[i, j, :, n:] = imag[first : first + rows]


def call(kernel, out_shapes, *operands, scratch=(), flops=0, smem=0, limit=24):
    whole = pl.BlockSpec(memory_space=pltpu.VMEM)
    scalars = pl.BlockSpec(memory_space=pltpu.SMEM)
    outs = [pltpu.VMEM(s, d) for s, d in out_shapes]
    operands = list(operands[:smem]) + [pltpu.with_memory_space_constraint(o, pltpu.VMEM) for o in operands[smem:]]
    result = pl.pallas_call(
        kernel,
        out_shape=outs,
        in_specs=[scalars] * smem + [whole] * (len(operands) - smem),
        out_specs=[whole] * len(outs),
        scratch_shapes=[pltpu.VMEM(s, d) for s, d in scratch],
        cost_estimate=pl.CostEstimate(flops=flops, transcendentals=0, bytes_accessed=1 << 20),
        compiler_params=pltpu.CompilerParams(vmem_limit_bytes=limit << 20),
    )(*operands)
    return result if len(outs) > 1 else result[0]


def fermi(index_values, scale):
    exponent = (index_values.astype(F32) - 128.0) / 24.0
    return scale / (1.0 + jnp.exp(exponent))


def shards(green_local, coupling, masks, incident, energy_index):
    count = green_local.shape[0]
    n = green_local.shape[3]
    modes = incident.shape[4]
    cols = 2 * modes
    devices = lax.axis_size("energy")
    ny, nx, nz = energy_grid(devices)
    at = lambda y, x, z: (y * nx + x) * nz + z
    along_z = [[at(y, x, z) for z in range(nz)] for y in range(ny) for x in range(nx)]
    along_yx = [[at(y, x, z) for y in range(ny) for x in range(nx)] for z in range(nz)]
    along_x = [[at(y, x, z) for x in range(nx)] for y in range(ny) for z in range(nz)]
    along_yz = [[at(y, x, z) for y in range(ny) for z in range(nz)] for x in range(nx)]
    rows = coupling.shape[1]
    tile = n // masks.shape[1]
    vec = (n, cols)
    mat = (2, n, n)
    unit = 2 * n * n * cols

    some = exchange(jnp.tile(coupling[0], (nz, 1)), along_z)
    by_row = jnp.repeat(masks[0].astype(BF16), tile, axis=0)
    first_row = (lax.axis_index("energy") // nz) * nz * rows
    here = lax.dynamic_slice_in_dim(by_row, first_row, nz * rows, 0)
    some = some * jnp.repeat(here, tile, axis=1)

    core = lax.rem(lax.axis_index("slab"), 2)
    own = green_local[:, 0]
    green = ordered(core, pick(own, core), swap(pick(own, 1 - core)))
    own = incident[:, 0].reshape(count, n, cols)
    source = ordered(core, pick(own, core), swap(pick(own, 1 - core)))
    some, green, source = lax.optimization_barrier((jnp.tile(some, (ny * nx, 1)), green, source))
    whole = exchange(some, along_yx)
    first = jnp.stack([apply(green[s, 0], green[s, 1], source[s]) for s in range(2)]).astype(BF16)
    following = chip_hop(first[0], -1)
    c = ordered(core, whole, swap(whole))
    ct = c.transpose(0, 2, 1)

    hops = lax.axis_size("slab") // 2 - 1
    base, start, send = call(
        begin_kernel, [(vec, F32), (vec, F32), (vec, BF16)], green, c, ct, source, first, following, flops=8 * unit
    )
    flux = chip_hop(send, 1)
    step_a, through = call(
        compose_kernel, [(mat, BF16), (mat, BF16)], green, ct, scratch=[(mat, BF16)], flops=16 * n**3
    )
    for _ in range(hops - 1):
        send = call(hop_kernel, [(vec, BF16)], through, start, flux, flops=2 * unit)
        flux = chip_hop(send, 1)
    back = call(
        compose_back_kernel, [(mat, BF16)], green, c, scratch=[(mat, BF16), (mat, BF16)], flops=16 * n**3
    )
    left, start, send = call(
        turn_kernel, [((2, *vec), F32), (vec, F32), (vec, BF16)], green, c, step_a, source, base, flux, flops=7 * unit
    )
    arrived = chip_hop(send, -1)
    for _ in range(hops - 1):
        send = call(hop_kernel, [(vec, BF16)], back, start, arrived, flops=2 * unit)
        arrived = chip_hop(send, -1)
    which = core.reshape(1)
    kept, send = call(
        finish_kernel, [(vec, BF16), (vec, BF16)], which, green, c, left, arrived, smem=1, flops=6 * unit
    )

    got = swap(send)
    weights = fermi(energy_index, 4.0 / (count * devices * modes))
    partial = call(
        density_kernel, [((nx, ny, nz * rows, 2 * n), BF16)], which, weights, kept, got, smem=2, flops=8 * unit
    )
    parts = exchange(partial, along_x)
    summed = jnp.sum(parts.astype(F32), axis=0).astype(BF16)
    parts = exchange(summed.reshape(ny * nz, rows, 2 * n), along_yz)
    density = jnp.sum(parts.astype(F32), axis=0).reshape(1, rows, 2, n)

    wave = ordered(core, kept, got)
    outflow = jnp.stack([mul(whole.T, wave[e]) for e in range(count)]).astype(BF16)
    shape = (count, 1, n, 2, modes)
    return (wave.reshape(shape), outflow.reshape(shape), density)


def solution(mesh):
    return jax.shard_map(
        shards,
        mesh=mesh,
        in_specs=(
            P("energy", "slab", None, None, None),
            P("slab", "energy", None),
            P("slab", None, None),
            P("energy", "slab", None, None, None),
            P("energy"),
        ),
        out_specs=(
            P("energy", "slab", None, None, None),
            P("energy", "slab", None, None, None),
            P("slab", "energy", None, None),
        ),
        check_vma=False,
    )
```

```python
import jax
import jax.numpy as jnp
from jax import lax
from jax.experimental import pallas as pl
from jax.experimental.pallas import tpu as pltpu
from jax.sharding import PartitionSpec as P

BF16 = jnp.bfloat16
F32 = jnp.float32


def chip_hop(block, distance):
    size = lax.axis_size("slab")
    route = [(i, i + 2 * distance) for i in range(size) if 0 <= i + 2 * distance < size]
    return lax.ppermute(block, "slab", route)


def swap(block):
    route = [(i, i ^ 1) for i in range(lax.axis_size("slab"))]
    return lax.ppermute(block, "slab", route)


def pick(blocks, index):
    return lax.dynamic_index_in_dim(blocks, index, 0, keepdims=False)


def ordered(core, kept, got):
    even = core == 0
    return jnp.stack([jnp.where(even, kept, got), jnp.where(even, got, kept)])


def exchange(block, groups):
    return lax.all_to_all(block, "energy", 0, 0, axis_index_groups=groups, tiled=True)


def energy_grid(devices):
    return (2, 2, 2) if devices == 8 else (2, 4, devices // 8)


def mul(left, right):
    return lax.dot_general(left, right, (((1,), (0,)), ((), ())), preferred_element_type=F32)


def mul_transposed(left, right):
    return lax.dot_general(left, right, (((1,), (1,)), ((), ())), preferred_element_type=F32)


def turned(vector):
    k = vector.shape[1] // 2
    return jnp.concatenate([-vector[:, k:], vector[:, :k]], axis=1)


def apply(real, imag, vector):
    return mul(real, vector) + mul(imag, turned(vector))


def product(left, right, out):
    lr, li, rr, ri = left[0], left[1], right[0], right[1]
    out[0] = (mul(lr, rr) - mul(li, ri)).astype(BF16)
    out[1] = (mul(lr, ri) + mul(li, rr)).astype(BF16)


def split_kernel(core, own, block):
    block[...] = own[1 - core[0]]


def first_kernel(core, own_g, got_g, own_s, got_s, g, src, first, send):
    here = core[0]
    g[here] = own_g[here]
    g[1 - here] = got_g[...]
    src[here] = own_s[here]
    src[1 - here] = got_s[...]
    field = apply(g[0, 0], g[0, 1], src[0]).astype(BF16)
    send[...] = field
    first[...] = apply(g[1, 0], g[1, 1], src[1]).astype(BF16)


def begin_kernel(core, own_c, got_c, g, src, first, following, c, ct, base, start, send):
    outer, inner, rows, _ = own_c.shape
    here = core[0]
    for i in range(outer):
        for j in range(inner):
            at = (j * outer + i) * rows
            c[here, at : at + rows] = own_c[i, j]
            c[1 - here, at : at + rows] = got_c[i, j]
    base_a = src[0].astype(F32) + mul(c[0], first[...])
    base[...] = base_a
    ct[0] = c[0].T
    ct[1] = c[1].T
    field = apply(g[0, 0], g[0, 1], base_a.astype(BF16)).astype(BF16)
    summed = src[1].astype(F32) + mul(c[1], following[...]) + mul(ct[0], field)
    field = apply(g[1, 0], g[1, 1], summed.astype(BF16)).astype(BF16)
    flux = mul(ct[1], field)
    start[...] = flux
    send[...] = flux.astype(BF16)


def compose_kernel(g, ct, step_a, through, step_b):
    step_a[0] = mul(ct[0], g[0, 0]).astype(BF16)
    step_a[1] = mul(ct[0], g[0, 1]).astype(BF16)
    step_b[0] = mul(ct[1], g[1, 0]).astype(BF16)
    step_b[1] = mul(ct[1], g[1, 1]).astype(BF16)
    product(step_b, step_a, through)


def compose_back_kernel(g, c, back_a, back_b, back):
    back_a[0] = mul(g[0, 0], c[0]).astype(BF16)
    back_a[1] = mul(g[0, 1], c[0]).astype(BF16)
    back_b[0] = mul(g[1, 0], c[1]).astype(BF16)
    back_b[1] = mul(g[1, 1], c[1]).astype(BF16)
    product(back_a, back_b, back)


def compose_turn_kernel(g, step_a, back_a, src, base, to_b, to_a, field_b, field_a):
    gbr, gbi = g[1, 0], g[1, 1]
    sr, si = step_a[0], step_a[1]
    to_b[0] = (mul(gbr, sr) - mul(gbi, si)).astype(BF16)
    to_b[1] = (mul(gbr, si) + mul(gbi, sr)).astype(BF16)
    ar, ai = back_a[0], back_a[1]
    br, bi = to_b[0], to_b[1]
    to_a[0] = (g[0, 0].astype(F32) + mul(ar, br) - mul(ai, bi)).astype(BF16)
    to_a[1] = (g[0, 1].astype(F32) + mul(ar, bi) + mul(ai, br)).astype(BF16)
    flux_a = apply(sr, si, base[...].astype(BF16))
    here = apply(gbr, gbi, (src[1].astype(F32) + flux_a).astype(BF16))
    field_b[...] = here
    field_a[...] = apply(g[0, 0], g[0, 1], src[0]) + apply(ar, ai, here.astype(BF16))


def hop_kernel(matrix, start, arrived, send):
    send[...] = (start[...] + apply(matrix[0], matrix[1], arrived[...])).astype(BF16)


def turn_kernel(to_a, to_b, field_a, field_b, flux, start, end, send):
    arrived = flux[...]
    wave = field_a[...] + apply(to_a[0], to_a[1], arrived)
    start[...] = wave
    send[...] = wave.astype(BF16)
    end[...] = field_b[...] + apply(to_b[0], to_b[1], arrived)


def finish_kernel(core, back, back_b, start, end, arrived, keep, send):
    wave_a = (start[...] + apply(back[0], back[1], arrived[...])).astype(BF16)
    wave_b = (end[...] + apply(back_b[0], back_b[1], arrived[...])).astype(BF16)

    @pl.when(core[0] == 0)
    def _():
        keep[...] = wave_a
        send[...] = wave_b

    @pl.when(core[0] != 0)
    def _():
        keep[...] = wave_b
        send[...] = wave_a


def density_kernel(core, weights, kept, got, out):
    n, _ = kept.shape
    outer, inner, rows, _ = out.shape
    here = weights[core[0]]
    there = weights[1 - core[0]]
    real = jnp.zeros((n, n), F32)
    imag = jnp.zeros((n, n), F32)
    for weight, wave in ((here, kept), (there, got)):
        w = wave[...]
        scaled = (w.astype(F32) * weight).astype(BF16)
        real = real + mul_transposed(scaled, w)
        imag = imag + mul_transposed(scaled, turned(w))
    real = real.astype(BF16)
    imag = imag.astype(BF16)
    for i in range(outer):
        for j in range(inner):
            first = (j * outer + i) * rows
            out[i, j, :, :n] = real[first : first + rows]
            out[i, j, :, n:] = imag[first : first + rows]


def call(kernel, out_shapes, *operands, scratch=(), flops=0, smem=0, limit=24):
    whole = pl.BlockSpec(memory_space=pltpu.VMEM)
    scalars = pl.BlockSpec(memory_space=pltpu.SMEM)
    outs = [pltpu.VMEM(s, d) for s, d in out_shapes]
    operands = list(operands[:smem]) + [pltpu.with_memory_space_constraint(o, pltpu.VMEM) for o in operands[smem:]]
    result = pl.pallas_call(
        kernel,
        out_shape=outs,
        in_specs=[scalars] * smem + [whole] * (len(operands) - smem),
        out_specs=[whole] * len(outs),
        scratch_shapes=[pltpu.VMEM(s, d) for s, d in scratch],
        cost_estimate=pl.CostEstimate(flops=flops, transcendentals=0, bytes_accessed=1 << 20),
        compiler_params=pltpu.CompilerParams(vmem_limit_bytes=limit << 20),
    )(*operands)
    return result if len(outs) > 1 else result[0]


def fermi(index_values, scale):
    exponent = (index_values.astype(F32) - 128.0) / 24.0
    return scale / (1.0 + jnp.exp(exponent))


def shards(green_local, coupling, masks, incident, energy_index):
    count = green_local.shape[0]
    n = green_local.shape[3]
    modes = incident.shape[4]
    cols = 2 * modes
    devices = lax.axis_size("energy")
    ny, nx, nz = energy_grid(devices)
    at = lambda y, x, z: (y * nx + x) * nz + z
    along_x = [[at(y, x, z) for x in range(nx)] for y in range(ny) for z in range(nz)]
    along_yz = [[at(y, x, z) for y in range(ny) for z in range(nz)] for x in range(nx)]
    rows = coupling.shape[1]
    tile = n // masks.shape[1]
    vec = (n, cols)
    mat = (2, n, n)
    unit = 2 * n * n * cols

    core = lax.rem(lax.axis_index("slab"), 2)
    which = core.reshape(1)

    some = jnp.tile(coupling[0], (ny * nz, 1))
    some, green_local, incident = lax.optimization_barrier((some, green_local, incident))
    own_g, own_s = green_local[:, 0], incident[:, 0].reshape(count, n, cols)
    some = exchange(some, along_yz)
    by_row = jnp.repeat(masks[0].astype(BF16), tile, axis=0).reshape(ny, nx, nz * rows, -1)
    here = lax.rem(lax.axis_index("energy") // nz, nx)
    here = lax.dynamic_index_in_dim(by_row, here, 1, keepdims=False)
    some = some.reshape(ny, nz * rows, n) * jnp.repeat(here, tile, axis=2)

    got_g = swap(call(split_kernel, [(mat, BF16)], which, own_g, smem=1))
    got_s = swap(call(split_kernel, [(vec, BF16)], which, own_s, smem=1))
    green, source, first, send = call(
        first_kernel,
        [((2, *mat), BF16), ((2, *vec), BF16), (vec, BF16), (vec, BF16)],
        which, own_g, got_g, own_s, got_s, smem=1, flops=4 * unit,
    )
    some = jnp.broadcast_to(some[None], (nx, *some.shape))
    some, send = lax.optimization_barrier((some, send))
    own_c = exchange(some, along_x)
    following = chip_hop(send, -1)
    got_c = swap(own_c)

    hops = lax.axis_size("slab") // 2 - 1
    c, ct, base, start, send = call(
        begin_kernel,
        [(mat, BF16), (mat, BF16), (vec, F32), (vec, F32), (vec, BF16)],
        which, own_c, got_c, green, source, first, following, smem=1, flops=8 * unit,
    )
    flux = chip_hop(send, 1)
    step_a, through = call(
        compose_kernel, [(mat, BF16), (mat, BF16)], green, ct, scratch=[(mat, BF16)], flops=16 * n**3
    )
    for _ in range(hops - 1):
        send = call(hop_kernel, [(vec, BF16)], through, start, flux, flops=2 * unit)
        flux = chip_hop(send, 1)
    back_a, back_b, back = call(compose_back_kernel, [(mat, BF16)] * 3, green, c, flops=16 * n**3)
    to_b, to_a, field_b, field_a = call(
        compose_turn_kernel,
        [(mat, BF16), (mat, BF16), (vec, F32), (vec, F32)],
        green, step_a, back_a, source, base, flops=16 * n**3 + 8 * unit,
    )
    start, end, send = call(
        turn_kernel, [(vec, F32), (vec, F32), (vec, BF16)], to_a, to_b, field_a, field_b, flux, flops=4 * unit
    )
    arrived = chip_hop(send, -1)
    for _ in range(hops - 1):
        send = call(hop_kernel, [(vec, BF16)], back, start, arrived, flops=2 * unit)
        arrived = chip_hop(send, -1)
    kept, send = call(
        finish_kernel, [(vec, BF16), (vec, BF16)], which, back, back_b, start, end, arrived, smem=1, flops=4 * unit
    )

    got = swap(send)
    weights = fermi(energy_index, 4.0 / (count * devices * modes))
    partial = call(
        density_kernel, [((nx, ny, nz * rows, 2 * n), BF16)], which, weights, kept, got, smem=2, flops=8 * unit
    )
    parts = exchange(partial, along_x)
    summed = jnp.sum(parts.astype(F32), axis=0).astype(BF16)
    parts = exchange(summed.reshape(ny * nz, rows, 2 * n), along_yz)
    density = jnp.sum(parts.astype(F32), axis=0).reshape(1, rows, 2, n)

    wave = ordered(core, kept, got)
    flow = pick(ct, core)
    outflow = jnp.stack([mul(flow, wave[e]) for e in range(count)]).astype(BF16)
    shape = (count, 1, n, 2, modes)
    return (wave.reshape(shape), outflow.reshape(shape), density)


def solution(mesh):
    return jax.shard_map(
        shards,
        mesh=mesh,
        in_specs=(
            P("energy", "slab", None, None, None),
            P("slab", "energy", None),
            P("slab", None, None),
            P("energy", "slab", None, None, None),
            P("energy"),
        ),
        out_specs=(
            P("energy", "slab", None, None, None),
            P("energy", "slab", None, None, None),
            P("slab", "energy", None, None),
        ),
        check_vma=False,
    )
```

```python
import jax
import jax.numpy as jnp
from jax import lax
from jax.experimental import pallas as pl
from jax.experimental.pallas import tpu as pltpu
from jax.sharding import PartitionSpec as P

BF16 = jnp.bfloat16
F32 = jnp.float32


def chip_hop(block, distance):
    size = lax.axis_size("slab")
    route = [(i, i + 2 * distance) for i in range(size) if 0 <= i + 2 * distance < size]
    return lax.ppermute(block, "slab", route)


def swap(block):
    route = [(i, i ^ 1) for i in range(lax.axis_size("slab"))]
    return lax.ppermute(block, "slab", route)


def pick(blocks, index):
    return lax.dynamic_index_in_dim(blocks, index, 0, keepdims=False)


def ordered(core, kept, got):
    even = core == 0
    return jnp.stack([jnp.where(even, kept, got), jnp.where(even, got, kept)])


def exchange(block, groups):
    return lax.all_to_all(block, "energy", 0, 0, axis_index_groups=groups, tiled=True)


def energy_grid(devices):
    return (2, 2, 2) if devices == 8 else (2, 4, devices // 8)


def mul(left, right):
    return lax.dot_general(left, right, (((1,), (0,)), ((), ())), preferred_element_type=F32)


def mul_transposed(left, right):
    return lax.dot_general(left, right, (((1,), (1,)), ((), ())), preferred_element_type=F32)


def turned(vector):
    k = vector.shape[1] // 2
    return jnp.concatenate([-vector[:, k:], vector[:, :k]], axis=1)


def apply(real, imag, vector):
    return mul(real, vector) + mul(imag, turned(vector))


def product(left, right, out):
    lr, li, rr, ri = left[0], left[1], right[0], right[1]
    out[0] = (mul(lr, rr) - mul(li, ri)).astype(BF16)
    out[1] = (mul(lr, ri) + mul(li, rr)).astype(BF16)


def rows_kernel(place, masks, rows, out):
    copies, count, n = out.shape
    blocks = masks.shape[1]
    tile = n // blocks
    here = (place[0] * count) // tile
    for j in range(blocks):
        at = slice(j * tile, (j + 1) * tile)
        present = masks[here, j].astype(F32)
        masked = (rows[:, at].astype(F32) * present).astype(BF16)
        for i in range(copies):
            out[i, :, at] = masked


def split_kernel(core, own, block):
    block[...] = own[1 - core[0]]


def first_kernel(core, own_g, got_g, own_s, got_s, g, src, first, send):
    here = core[0]
    g[here] = own_g[here]
    g[1 - here] = got_g[...]
    src[here] = own_s[here]
    src[1 - here] = got_s[...]
    field = apply(g[0, 0], g[0, 1], src[0]).astype(BF16)
    send[...] = field
    first[...] = apply(g[1, 0], g[1, 1], src[1]).astype(BF16)


def begin_kernel(core, own_c, got_c, g, src, first, following, c, ct, base, start, send):
    here = core[0]
    c[here] = own_c[...]
    c[1 - here] = got_c[...]
    base_a = src[0].astype(F32) + mul(c[0], first[...])
    base[...] = base_a
    ct[0] = c[0].T
    ct[1] = c[1].T
    field = apply(g[0, 0], g[0, 1], base_a.astype(BF16)).astype(BF16)
    summed = src[1].astype(F32) + mul(c[1], following[...]) + mul(ct[0], field)
    field = apply(g[1, 0], g[1, 1], summed.astype(BF16)).astype(BF16)
    flux = mul(ct[1], field)
    start[...] = flux
    send[...] = flux.astype(BF16)


def compose_kernel(g, ct, step_a, through, step_b):
    step_a[0] = mul(ct[0], g[0, 0]).astype(BF16)
    step_a[1] = mul(ct[0], g[0, 1]).astype(BF16)
    step_b[0] = mul(ct[1], g[1, 0]).astype(BF16)
    step_b[1] = mul(ct[1], g[1, 1]).astype(BF16)
    product(step_b, step_a, through)


def compose_back_kernel(g, c, back_a, back_b, back):
    back_a[0] = mul(g[0, 0], c[0]).astype(BF16)
    back_a[1] = mul(g[0, 1], c[0]).astype(BF16)
    back_b[0] = mul(g[1, 0], c[1]).astype(BF16)
    back_b[1] = mul(g[1, 1], c[1]).astype(BF16)
    product(back_a, back_b, back)


def compose_turn_kernel(g, step_a, back_a, src, base, to_b, to_a, field_b, field_a):
    gbr, gbi = g[1, 0], g[1, 1]
    sr, si = step_a[0], step_a[1]
    to_b[0] = (mul(gbr, sr) - mul(gbi, si)).astype(BF16)
    to_b[1] = (mul(gbr, si) + mul(gbi, sr)).astype(BF16)
    ar, ai = back_a[0], back_a[1]
    br, bi = to_b[0], to_b[1]
    to_a[0] = (g[0, 0].astype(F32) + mul(ar, br) - mul(ai, bi)).astype(BF16)
    to_a[1] = (g[0, 1].astype(F32) + mul(ar, bi) + mul(ai, br)).astype(BF16)
    flux_a = apply(sr, si, base[...].astype(BF16))
    here = apply(gbr, gbi, (src[1].astype(F32) + flux_a).astype(BF16))
    field_b[...] = here
    field_a[...] = apply(g[0, 0], g[0, 1], src[0]) + apply(ar, ai, here.astype(BF16))


def hop_kernel(matrix, start, arrived, send):
    send[...] = (start[...] + apply(matrix[0], matrix[1], arrived[...])).astype(BF16)


def turn_kernel(to_a, to_b, field_a, field_b, flux, start, end, send):
    arrived = flux[...]
    wave = field_a[...] + apply(to_a[0], to_a[1], arrived)
    start[...] = wave
    send[...] = wave.astype(BF16)
    end[...] = field_b[...] + apply(to_b[0], to_b[1], arrived)


def finish_kernel(core, back, back_b, start, end, arrived, keep, send):
    wave_a = (start[...] + apply(back[0], back[1], arrived[...])).astype(BF16)
    wave_b = (end[...] + apply(back_b[0], back_b[1], arrived[...])).astype(BF16)

    @pl.when(core[0] == 0)
    def _():
        keep[...] = wave_a
        send[...] = wave_b

    @pl.when(core[0] != 0)
    def _():
        keep[...] = wave_b
        send[...] = wave_a


def density_kernel(core, weights, kept, got, out):
    n, _ = kept.shape
    nx, near, ny, far, rows, _ = out.shape
    here = weights[core[0]]
    there = weights[1 - core[0]]
    real = jnp.zeros((n, n), F32)
    imag = jnp.zeros((n, n), F32)
    for weight, wave in ((here, kept), (there, got)):
        w = wave[...]
        scaled = (w.astype(F32) * weight).astype(BF16)
        real = real + mul_transposed(scaled, w)
        imag = imag + mul_transposed(scaled, turned(w))
    real = real.astype(BF16)
    imag = imag.astype(BF16)
    for y in range(ny):
        for x in range(nx):
            for h in range(far):
                for l in range(near):
                    at = (((y * nx + x) * far + h) * near + l) * rows
                    out[x, l, y, h, :, :n] = real[at : at + rows]
                    out[x, l, y, h, :, n:] = imag[at : at + rows]


def call(kernel, out_shapes, *operands, scratch=(), flops=0, smem=0, limit=24, placed=True):
    whole = pl.BlockSpec(memory_space=pltpu.VMEM)
    scalars = pl.BlockSpec(memory_space=pltpu.SMEM)
    outs = [pltpu.VMEM(s, d) if placed else jax.ShapeDtypeStruct(s, d) for s, d in out_shapes]
    operands = list(operands[:smem]) + [pltpu.with_memory_space_constraint(o, pltpu.VMEM) for o in operands[smem:]]
    result = pl.pallas_call(
        kernel,
        out_shape=outs,
        in_specs=[scalars] * smem + [whole] * (len(operands) - smem),
        out_specs=[whole] * len(outs),
        scratch_shapes=[pltpu.VMEM(s, d) for s, d in scratch],
        cost_estimate=pl.CostEstimate(flops=flops, transcendentals=0, bytes_accessed=1 << 20),
        compiler_params=pltpu.CompilerParams(vmem_limit_bytes=limit << 20),
    )(*operands)
    return result if len(outs) > 1 else result[0]


def fermi(index_values, scale):
    exponent = (index_values.astype(F32) - 128.0) / 24.0
    return scale / (1.0 + jnp.exp(exponent))


def shards(green_local, coupling, masks, incident, energy_index):
    count = green_local.shape[0]
    n = green_local.shape[3]
    modes = incident.shape[4]
    cols = 2 * modes
    devices = lax.axis_size("energy")
    ny, nx, nz = energy_grid(devices)
    near, far = 2, nz // 2
    at = lambda y, x, h, l: ((y * nx + x) * far + h) * near + l
    along_xl = [[at(y, x, h, l) for x in range(nx) for l in range(near)] for y in range(ny) for h in range(far)]
    along_yh = [[at(y, x, h, l) for y in range(ny) for h in range(far)] for x in range(nx) for l in range(near)]
    rows = coupling.shape[1]
    tile = n // masks.shape[1]
    vec = (n, cols)
    mat = (2, n, n)
    unit = 2 * n * n * cols

    core = lax.rem(lax.axis_index("slab"), 2)
    which = core.reshape(1)

    place = lax.axis_index("energy").reshape(1)
    mine = call(
        rows_kernel, [((devices, rows, n), BF16)], place, masks[0], coupling[0], smem=2, placed=False
    )
    own_c = exchange(mine, None).reshape(n, n)
    own_g, own_s = green_local[:, 0], incident[:, 0].reshape(count, n, cols)

    got_g = swap(call(split_kernel, [(mat, BF16)], which, own_g, smem=1))
    got_s = swap(call(split_kernel, [(vec, BF16)], which, own_s, smem=1))
    green, source, first, send = call(
        first_kernel,
        [((2, *mat), BF16), ((2, *vec), BF16), (vec, BF16), (vec, BF16)],
        which, own_g, got_g, own_s, got_s, smem=1, flops=4 * unit,
    )
    following = chip_hop(send, -1)
    own_c, following = lax.optimization_barrier((own_c, following))
    got_c = swap(own_c)

    hops = lax.axis_size("slab") // 2 - 1
    c, ct, base, start, send = call(
        begin_kernel,
        [(mat, BF16), (mat, BF16), (vec, F32), (vec, F32), (vec, BF16)],
        which, own_c, got_c, green, source, first, following, smem=1, flops=8 * unit,
    )
    flux = chip_hop(send, 1)
    step_a, through = call(
        compose_kernel, [(mat, BF16), (mat, BF16)], green, ct, scratch=[(mat, BF16)], flops=16 * n**3
    )
    for _ in range(hops - 1):
        send = call(hop_kernel, [(vec, BF16)], through, start, flux, flops=2 * unit)
        flux = chip_hop(send, 1)
    back_a, back_b, back = call(compose_back_kernel, [(mat, BF16)] * 3, green, c, flops=16 * n**3)
    to_b, to_a, field_b, field_a = call(
        compose_turn_kernel,
        [(mat, BF16), (mat, BF16), (vec, F32), (vec, F32)],
        green, step_a, back_a, source, base, flops=16 * n**3 + 8 * unit,
    )
    start, end, send = call(
        turn_kernel, [(vec, F32), (vec, F32), (vec, BF16)], to_a, to_b, field_a, field_b, flux, flops=4 * unit
    )
    arrived = chip_hop(send, -1)
    for _ in range(hops - 1):
        send = call(hop_kernel, [(vec, BF16)], back, start, arrived, flops=2 * unit)
        arrived = chip_hop(send, -1)
    kept, send = call(
        finish_kernel, [(vec, BF16), (vec, BF16)], which, back, back_b, start, end, arrived, smem=1, flops=4 * unit
    )

    got = swap(send)
    weights = fermi(energy_index, 4.0 / (count * devices * modes))
    partial = call(
        density_kernel,
        [((nx, near, ny, far, rows, 2 * n), BF16)],
        which, weights, kept, got, smem=2, flops=8 * unit,
    )
    parts = exchange(partial.reshape(nx * near, ny * far, rows, 2 * n), along_xl)
    summed = jnp.sum(parts.astype(F32), axis=0).astype(BF16)
    parts = exchange(summed, along_yh)
    density = jnp.sum(parts.astype(F32), axis=0).reshape(1, rows, 2, n)

    wave = ordered(core, kept, got)
    flow = pick(ct, core)
    outflow = jnp.stack([mul(flow, wave[e]) for e in range(count)]).astype(BF16)
    shape = (count, 1, n, 2, modes)
    return (wave.reshape(shape), outflow.reshape(shape), density)


def solution(mesh):
    return jax.shard_map(
        shards,
        mesh=mesh,
        in_specs=(
            P("energy", "slab", None, None, None),
            P("slab", "energy", None),
            P("slab", None, None),
            P("energy", "slab", None, None, None),
            P("energy"),
        ),
        out_specs=(
            P("energy", "slab", None, None, None),
            P("energy", "slab", None, None, None),
            P("slab", "energy", None, None),
        ),
        check_vma=False,
    )
```

```python
import jax
import jax.numpy as jnp
from jax import lax
from jax.experimental import pallas as pl
from jax.experimental.pallas import tpu as pltpu
from jax.sharding import PartitionSpec as P

BF16 = jnp.bfloat16
F32 = jnp.float32


def chip_hop(block, distance):
    size = lax.axis_size("slab")
    route = [(i, i + 2 * distance) for i in range(size) if 0 <= i + 2 * distance < size]
    return lax.ppermute(block, "slab", route)


def swap(block):
    route = [(i, i ^ 1) for i in range(lax.axis_size("slab"))]
    return lax.ppermute(block, "slab", route)


def pick(blocks, index):
    return lax.dynamic_index_in_dim(blocks, index, 0, keepdims=False)


def ordered(core, kept, got):
    even = core == 0
    return jnp.stack([jnp.where(even, kept, got), jnp.where(even, got, kept)])


def exchange(block, groups):
    return lax.all_to_all(block, "energy", 0, 0, axis_index_groups=groups, tiled=True)


def energy_grid(devices):
    return (2, 2, 2) if devices == 8 else (2, 4, devices // 8)


def mul(left, right):
    return lax.dot_general(left, right, (((1,), (0,)), ((), ())), preferred_element_type=F32)


def mul_transposed(left, right):
    return lax.dot_general(left, right, (((1,), (1,)), ((), ())), preferred_element_type=F32)


def turned(vector):
    k = vector.shape[1] // 2
    return jnp.concatenate([-vector[:, k:], vector[:, :k]], axis=1)


def apply(real, imag, vector):
    return mul(real, vector) + mul(imag, turned(vector))


def product(left, right, out):
    lr, li, rr, ri = left[0], left[1], right[0], right[1]
    out[0] = (mul(lr, rr) - mul(li, ri)).astype(BF16)
    out[1] = (mul(lr, ri) + mul(li, rr)).astype(BF16)


def rows_kernel(place, masks, rows, out):
    copies, count, n = out.shape
    blocks = masks.shape[1]
    tile = n // blocks
    here = (place[0] * count) // tile
    for j in range(blocks):
        at = slice(j * tile, (j + 1) * tile)
        present = masks[here, j].astype(F32)
        masked = (rows[:, at].astype(F32) * present).astype(BF16)
        for i in range(copies):
            out[i, :, at] = masked


def split_kernel(core, own, block):
    block[...] = own[1 - core[0]]


def first_kernel(core, own_g, got_g, own_s, got_s, g, src, first, send):
    here = core[0]
    g[here] = own_g[here]
    g[1 - here] = got_g[...]
    src[here] = own_s[here]
    src[1 - here] = got_s[...]
    field = apply(g[0, 0], g[0, 1], src[0]).astype(BF16)
    send[...] = field
    first[...] = apply(g[1, 0], g[1, 1], src[1]).astype(BF16)


def compose(g, ct, step_a, through, step_b):
    step_a[0] = mul(ct[0], g[0, 0]).astype(BF16)
    step_a[1] = mul(ct[0], g[0, 1]).astype(BF16)
    step_b[0] = mul(ct[1], g[1, 0]).astype(BF16)
    step_b[1] = mul(ct[1], g[1, 1]).astype(BF16)
    product(step_b, step_a, through)


def begin_kernel(
    core, g_far, src_far, own_c, got_c, first, following,
    g, src, c, ct, base, start, send, step_a, through, step_b, g_sem, src_sem,
):
    src_copy = pltpu.make_async_copy(src_far, src, src_sem)
    g_copy = pltpu.make_async_copy(g_far, g, g_sem)
    src_copy.start()
    g_copy.start()
    here = core[0]
    c[here] = own_c[...]
    c[1 - here] = got_c[...]
    ct[0] = c[0].T
    ct[1] = c[1].T
    src_copy.wait()
    base_a = src[0].astype(F32) + mul(c[0], first[...])
    base[...] = base_a
    g_copy.wait()
    field = apply(g[0, 0], g[0, 1], base_a.astype(BF16)).astype(BF16)
    summed = src[1].astype(F32) + mul(c[1], following[...]) + mul(ct[0], field)
    field = apply(g[1, 0], g[1, 1], summed.astype(BF16)).astype(BF16)
    flux = mul(ct[1], field)
    start[...] = flux
    send[...] = flux.astype(BF16)

    @pl.when(here == 1)
    def _():
        compose(g, ct, step_a, through, step_b)


def compose_kernel(core, g, ct, step_a_in, through_in, step_a, through, step_b):
    @pl.when(core[0] == 0)
    def _():
        compose(g, ct, step_a, through, step_b)


def compose_back_kernel(g, c, back_a, back_b, back):
    back_a[0] = mul(g[0, 0], c[0]).astype(BF16)
    back_a[1] = mul(g[0, 1], c[0]).astype(BF16)
    back_b[0] = mul(g[1, 0], c[1]).astype(BF16)
    back_b[1] = mul(g[1, 1], c[1]).astype(BF16)
    product(back_a, back_b, back)


def compose_turn_kernel(g, step_a, back_a, src, base, to_b, to_a, field_b, field_a):
    gbr, gbi = g[1, 0], g[1, 1]
    sr, si = step_a[0], step_a[1]
    to_b[0] = (mul(gbr, sr) - mul(gbi, si)).astype(BF16)
    to_b[1] = (mul(gbr, si) + mul(gbi, sr)).astype(BF16)
    ar, ai = back_a[0], back_a[1]
    br, bi = to_b[0], to_b[1]
    to_a[0] = (g[0, 0].astype(F32) + mul(ar, br) - mul(ai, bi)).astype(BF16)
    to_a[1] = (g[0, 1].astype(F32) + mul(ar, bi) + mul(ai, br)).astype(BF16)
    flux_a = apply(sr, si, base[...].astype(BF16))
    here = apply(gbr, gbi, (src[1].astype(F32) + flux_a).astype(BF16))
    field_b[...] = here
    field_a[...] = apply(g[0, 0], g[0, 1], src[0]) + apply(ar, ai, here.astype(BF16))


def hop_kernel(matrix, start, arrived, send):
    send[...] = (start[...] + apply(matrix[0], matrix[1], arrived[...])).astype(BF16)


def turn_kernel(to_a, to_b, field_a, field_b, flux, start, end, send):
    arrived = flux[...]
    wave = field_a[...] + apply(to_a[0], to_a[1], arrived)
    start[...] = wave
    send[...] = wave.astype(BF16)
    end[...] = field_b[...] + apply(to_b[0], to_b[1], arrived)


def finish_kernel(core, back, back_b, start, end, arrived, keep, send):
    wave_a = (start[...] + apply(back[0], back[1], arrived[...])).astype(BF16)
    wave_b = (end[...] + apply(back_b[0], back_b[1], arrived[...])).astype(BF16)

    @pl.when(core[0] == 0)
    def _():
        keep[...] = wave_a
        send[...] = wave_b

    @pl.when(core[0] != 0)
    def _():
        keep[...] = wave_b
        send[...] = wave_a


def density_kernel(core, weights, kept, got, out):
    n, _ = kept.shape
    outer, inner, rows, _ = out.shape
    here = weights[core[0]]
    there = weights[1 - core[0]]
    real = jnp.zeros((n, n), F32)
    imag = jnp.zeros((n, n), F32)
    for weight, wave in ((here, kept), (there, got)):
        w = wave[...]
        scaled = (w.astype(F32) * weight).astype(BF16)
        real = real + mul_transposed(scaled, w)
        imag = imag + mul_transposed(scaled, turned(w))
    real = real.astype(BF16)
    imag = imag.astype(BF16)
    for i in range(outer):
        for j in range(inner):
            first = (j * outer + i) * rows
            out[i, j, :, :n] = real[first : first + rows]
            out[i, j, :, n:] = imag[first : first + rows]


def call(kernel, out_shapes, *operands, scratch=(), flops=0, smem=0, far=0, plain=0, aliases=None):
    whole = pl.BlockSpec(memory_space=pltpu.VMEM)
    specs = [pl.BlockSpec(memory_space=pltpu.SMEM)] * smem + [pl.BlockSpec(memory_space=pltpu.HBM)] * far
    outs = [pltpu.VMEM(s, d) if i >= plain else jax.ShapeDtypeStruct(s, d) for i, (s, d) in enumerate(out_shapes)]
    first = smem + far
    space = lambda i: pltpu.HBM if i < first else pltpu.VMEM
    operands = [
        o if i < smem else pltpu.with_memory_space_constraint(o, space(i)) for i, o in enumerate(operands)
    ]
    result = pl.pallas_call(
        kernel,
        out_shape=outs,
        in_specs=specs + [whole] * (len(operands) - first),
        out_specs=[whole] * len(outs),
        scratch_shapes=list(scratch),
        cost_estimate=pl.CostEstimate(flops=flops, transcendentals=0, bytes_accessed=1 << 20),
        compiler_params=pltpu.CompilerParams(vmem_limit_bytes=24 << 20),
        input_output_aliases=aliases or {},
    )(*operands)
    return result if len(outs) > 1 else result[0]


def fermi(index_values, scale):
    exponent = (index_values.astype(F32) - 128.0) / 24.0
    return scale / (1.0 + jnp.exp(exponent))


def shards(green_local, coupling, masks, incident, energy_index):
    count = green_local.shape[0]
    n = green_local.shape[3]
    modes = incident.shape[4]
    cols = 2 * modes
    devices = lax.axis_size("energy")
    ny, nx, nz = energy_grid(devices)
    at = lambda y, x, z: (y * nx + x) * nz + z
    along_x = [[at(y, x, z) for x in range(nx)] for y in range(ny) for z in range(nz)]
    along_yz = [[at(y, x, z) for y in range(ny) for z in range(nz)] for x in range(nx)]
    rows = coupling.shape[1]
    tile = n // masks.shape[1]
    vec = (n, cols)
    mat = (2, n, n)
    unit = 2 * n * n * cols

    core = lax.rem(lax.axis_index("slab"), 2)
    which = core.reshape(1)

    place = lax.axis_index("energy").reshape(1)
    mine = call(
        rows_kernel, [((devices, rows, n), BF16)], place, masks[0], coupling[0], smem=2, plain=1
    )
    own_c = exchange(mine, None).reshape(n, n)
    own_g, own_s = green_local[:, 0], incident[:, 0].reshape(count, n, cols)

    got_g = swap(call(split_kernel, [(mat, BF16)], which, own_g, smem=1))
    got_s = swap(call(split_kernel, [(vec, BF16)], which, own_s, smem=1))
    green, source, first, send = call(
        first_kernel,
        [((2, *mat), BF16), ((2, *vec), BF16), (vec, BF16), (vec, BF16)],
        which, own_g, got_g, own_s, got_s, smem=1, plain=2, flops=4 * unit,
    )
    following = chip_hop(send, -1)
    own_c, following = lax.optimization_barrier((own_c, following))
    got_c = swap(own_c)

    hops = lax.axis_size("slab") // 2 - 1
    green, source, c, ct, base, start, send, step_a, through = call(
        begin_kernel,
        [((2, *mat), BF16), ((2, *vec), BF16), (mat, BF16), (mat, BF16), (vec, F32), (vec, F32), (vec, BF16)]
        + [(mat, BF16)] * 2,
        which, green, source, own_c, got_c, first, following,
        smem=1, far=2, scratch=[pltpu.VMEM(mat, BF16)] + [pltpu.SemaphoreType.DMA(())] * 2, flops=8 * unit,
    )
    flux = chip_hop(send, 1)
    step_a, through = call(
        compose_kernel, [(mat, BF16), (mat, BF16)], which, green, ct, step_a, through,
        smem=1, scratch=[pltpu.VMEM(mat, BF16)], flops=16 * n**3, aliases={3: 0, 4: 1},
    )
    for _ in range(hops - 1):
        send = call(hop_kernel, [(vec, BF16)], through, start, flux, flops=2 * unit)
        flux = chip_hop(send, 1)
    back_a, back_b, back = call(compose_back_kernel, [(mat, BF16)] * 3, green, c, flops=16 * n**3)
    to_b, to_a, field_b, field_a = call(
        compose_turn_kernel,
        [(mat, BF16), (mat, BF16), (vec, F32), (vec, F32)],
        green, step_a, back_a, source, base, flops=16 * n**3 + 8 * unit,
    )
    start, end, send = call(
        turn_kernel, [(vec, F32), (vec, F32), (vec, BF16)], to_a, to_b, field_a, field_b, flux, flops=4 * unit
    )
    arrived = chip_hop(send, -1)
    for _ in range(hops - 1):
        send = call(hop_kernel, [(vec, BF16)], back, start, arrived, flops=2 * unit)
        arrived = chip_hop(send, -1)
    kept, send = call(
        finish_kernel, [(vec, BF16), (vec, BF16)], which, back, back_b, start, end, arrived, smem=1, flops=4 * unit
    )

    got = swap(send)
    weights = fermi(energy_index, 4.0 / (count * devices * modes))
    partial = call(
        density_kernel, [((nx, ny, nz * rows, 2 * n), BF16)], which, weights, kept, got, smem=2, flops=8 * unit
    )
    parts = exchange(partial, along_x)
    summed = jnp.sum(parts.astype(F32), axis=0).astype(BF16)
    parts = exchange(summed.reshape(ny * nz, rows, 2 * n), along_yz)
    density = jnp.sum(parts.astype(F32), axis=0).reshape(1, rows, 2, n)

    wave = ordered(core, kept, got)
    flow = pick(ct, core)
    outflow = jnp.stack([mul(flow, wave[e]) for e in range(count)]).astype(BF16)
    shape = (count, 1, n, 2, modes)
    return (wave.reshape(shape), outflow.reshape(shape), density)


def solution(mesh):
    return jax.shard_map(
        shards,
        mesh=mesh,
        in_specs=(
            P("energy", "slab", None, None, None),
            P("slab", "energy", None),
            P("slab", None, None),
            P("energy", "slab", None, None, None),
            P("energy"),
        ),
        out_specs=(
            P("energy", "slab", None, None, None),
            P("energy", "slab", None, None, None),
            P("slab", "energy", None, None),
        ),
        check_vma=False,
    )
```

```python
import jax
import jax.numpy as jnp
from jax import lax
from jax.experimental import pallas as pl
from jax.experimental.pallas import tpu as pltpu
from jax.sharding import PartitionSpec as P

BF16 = jnp.bfloat16
F32 = jnp.float32


def chip_hop(block, distance):
    size = lax.axis_size("slab")
    route = [(i, i + 2 * distance) for i in range(size) if 0 <= i + 2 * distance < size]
    return lax.ppermute(block, "slab", route)


def swap(block):
    route = [(i, i ^ 1) for i in range(lax.axis_size("slab"))]
    return lax.ppermute(block, "slab", route)


def pick(blocks, index):
    return lax.dynamic_index_in_dim(blocks, index, 0, keepdims=False)


def ordered(core, kept, got):
    even = core == 0
    return jnp.stack([jnp.where(even, kept, got), jnp.where(even, got, kept)])


def exchange(block, groups):
    return lax.all_to_all(block, "energy", 0, 0, axis_index_groups=groups, tiled=True)


def energy_grid(devices):
    return (2, 2, 2) if devices == 8 else (2, 4, devices // 8)


def mul(left, right):
    return lax.dot_general(left, right, (((1,), (0,)), ((), ())), preferred_element_type=F32)


def mul_transposed(left, right):
    return lax.dot_general(left, right, (((1,), (1,)), ((), ())), preferred_element_type=F32)


def turned(vector):
    k = vector.shape[1] // 2
    return jnp.concatenate([-vector[:, k:], vector[:, :k]], axis=1)


def apply(real, imag, vector):
    return mul(real, vector) + mul(imag, turned(vector))


def product(left, right, out):
    lr, li, rr, ri = left[0], left[1], right[0], right[1]
    out[0] = (mul(lr, rr) - mul(li, ri)).astype(BF16)
    out[1] = (mul(lr, ri) + mul(li, rr)).astype(BF16)


def rows_kernel(place, masks, rows, out):
    copies, count, n = out.shape
    blocks = masks.shape[1]
    tile = n // blocks
    here = (place[0] * count) // tile
    for j in range(blocks):
        at = slice(j * tile, (j + 1) * tile)
        present = masks[here, j].astype(F32)
        masked = (rows[:, at].astype(F32) * present).astype(BF16)
        for i in range(copies):
            out[i, :, at] = masked


def split_kernel(core, own, block):
    block[...] = own[1 - core[0]]


def first_kernel(g, src, here, there):
    here[...] = apply(g[0, 0], g[0, 1], src[0]).astype(BF16)
    there[...] = apply(g[1, 0], g[1, 1], src[1]).astype(BF16)


def begin_kernel(
    core, own_g, got_g, own_s, got_s, own_c, got_c, own_first, got_first, next_0, next_1,
    g, src, c, ct, base, start, send, sems,
):
    here = core[0]
    copies = [
        pltpu.make_async_copy(own_s.at[here], src.at[here], sems.at[0]),
        pltpu.make_async_copy(got_s, src.at[1 - here], sems.at[1]),
        pltpu.make_async_copy(own_g.at[here], g.at[here], sems.at[2]),
        pltpu.make_async_copy(got_g, g.at[1 - here], sems.at[3]),
    ]
    for copy in copies:
        copy.start()
    c[here] = own_c[...]
    c[1 - here] = got_c[...]
    ct[0] = c[0].T
    ct[1] = c[1].T
    first = jnp.where(here == 0, got_first[...], own_first[...])
    following = next_0[...] + next_1[...]
    copies[0].wait()
    copies[1].wait()
    base_a = src[0].astype(F32) + mul(c[0], first)
    base[...] = base_a
    copies[2].wait()
    copies[3].wait()
    field = apply(g[0, 0], g[0, 1], base_a.astype(BF16)).astype(BF16)
    summed = src[1].astype(F32) + mul(c[1], following) + mul(ct[0], field)
    field = apply(g[1, 0], g[1, 1], summed.astype(BF16)).astype(BF16)
    flux = mul(ct[1], field)
    start[...] = flux
    send[...] = flux.astype(BF16)


def compose_kernel(g, ct, step_a, through, step_b):
    step_a[0] = mul(ct[0], g[0, 0]).astype(BF16)
    step_a[1] = mul(ct[0], g[0, 1]).astype(BF16)
    step_b[0] = mul(ct[1], g[1, 0]).astype(BF16)
    step_b[1] = mul(ct[1], g[1, 1]).astype(BF16)
    product(step_b, step_a, through)


def compose_back_kernel(g, c, back_a, back_b, back):
    back_a[0] = mul(g[0, 0], c[0]).astype(BF16)
    back_a[1] = mul(g[0, 1], c[0]).astype(BF16)
    back_b[0] = mul(g[1, 0], c[1]).astype(BF16)
    back_b[1] = mul(g[1, 1], c[1]).astype(BF16)
    product(back_a, back_b, back)


def compose_turn_kernel(g, step_a, back_a, src, base, to_b, to_a, field_b, field_a):
    gbr, gbi = g[1, 0], g[1, 1]
    sr, si = step_a[0], step_a[1]
    to_b[0] = (mul(gbr, sr) - mul(gbi, si)).astype(BF16)
    to_b[1] = (mul(gbr, si) + mul(gbi, sr)).astype(BF16)
    ar, ai = back_a[0], back_a[1]
    br, bi = to_b[0], to_b[1]
    to_a[0] = (g[0, 0].astype(F32) + mul(ar, br) - mul(ai, bi)).astype(BF16)
    to_a[1] = (g[0, 1].astype(F32) + mul(ar, bi) + mul(ai, br)).astype(BF16)
    flux_a = apply(sr, si, base[...].astype(BF16))
    here = apply(gbr, gbi, (src[1].astype(F32) + flux_a).astype(BF16))
    field_b[...] = here
    field_a[...] = apply(g[0, 0], g[0, 1], src[0]) + apply(ar, ai, here.astype(BF16))


def hop_kernel(matrix, start, arrived, send):
    send[...] = (start[...] + apply(matrix[0], matrix[1], arrived[...])).astype(BF16)


def turn_kernel(to_a, to_b, field_a, field_b, flux, start, end, send):
    arrived = flux[...]
    wave = field_a[...] + apply(to_a[0], to_a[1], arrived)
    start[...] = wave
    send[...] = wave.astype(BF16)
    end[...] = field_b[...] + apply(to_b[0], to_b[1], arrived)


def finish_kernel(core, back, back_b, start, end, arrived, keep, send):
    wave_a = (start[...] + apply(back[0], back[1], arrived[...])).astype(BF16)
    wave_b = (end[...] + apply(back_b[0], back_b[1], arrived[...])).astype(BF16)

    @pl.when(core[0] == 0)
    def _():
        keep[...] = wave_a
        send[...] = wave_b

    @pl.when(core[0] != 0)
    def _():
        keep[...] = wave_b
        send[...] = wave_a


def density_kernel(core, weights, kept, got, out):
    n, _ = kept.shape
    outer, inner, rows, _ = out.shape
    here = weights[core[0]]
    there = weights[1 - core[0]]
    real = jnp.zeros((n, n), F32)
    imag = jnp.zeros((n, n), F32)
    for weight, wave in ((here, kept), (there, got)):
        w = wave[...]
        scaled = (w.astype(F32) * weight).astype(BF16)
        real = real + mul_transposed(scaled, w)
        imag = imag + mul_transposed(scaled, turned(w))
    real = real.astype(BF16)
    imag = imag.astype(BF16)
    for i in range(outer):
        for j in range(inner):
            first = (j * outer + i) * rows
            out[i, j, :, :n] = real[first : first + rows]
            out[i, j, :, n:] = imag[first : first + rows]


def call(kernel, out_shapes, *operands, scratch=(), flops=0, smem=0, far=0, plain=0):
    whole = pl.BlockSpec(memory_space=pltpu.VMEM)
    specs = [pl.BlockSpec(memory_space=pltpu.SMEM)] * smem + [pl.BlockSpec(memory_space=pltpu.HBM)] * far
    outs = [pltpu.VMEM(s, d) if i >= plain else jax.ShapeDtypeStruct(s, d) for i, (s, d) in enumerate(out_shapes)]
    first = smem + far
    space = lambda i: pltpu.HBM if i < first else pltpu.VMEM
    operands = [
        o if i < smem else pltpu.with_memory_space_constraint(o, space(i)) for i, o in enumerate(operands)
    ]
    result = pl.pallas_call(
        kernel,
        out_shape=outs,
        in_specs=specs + [whole] * (len(operands) - first),
        out_specs=[whole] * len(outs),
        scratch_shapes=list(scratch),
        cost_estimate=pl.CostEstimate(flops=flops, transcendentals=0, bytes_accessed=1 << 20),
        compiler_params=pltpu.CompilerParams(vmem_limit_bytes=24 << 20),
    )(*operands)
    return result if len(outs) > 1 else result[0]


def fermi(index_values, scale):
    exponent = (index_values.astype(F32) - 128.0) / 24.0
    return scale / (1.0 + jnp.exp(exponent))


def shards(green_local, coupling, masks, incident, energy_index):
    count = green_local.shape[0]
    n = green_local.shape[3]
    modes = incident.shape[4]
    cols = 2 * modes
    devices = lax.axis_size("energy")
    ny, nx, nz = energy_grid(devices)
    at = lambda y, x, z: (y * nx + x) * nz + z
    along_x = [[at(y, x, z) for x in range(nx)] for y in range(ny) for z in range(nz)]
    along_yz = [[at(y, x, z) for y in range(ny) for z in range(nz)] for x in range(nx)]
    rows = coupling.shape[1]
    tile = n // masks.shape[1]
    vec = (n, cols)
    mat = (2, n, n)
    unit = 2 * n * n * cols

    core = lax.rem(lax.axis_index("slab"), 2)
    which = core.reshape(1)

    place = lax.axis_index("energy").reshape(1)
    mine = call(
        rows_kernel, [((devices, rows, n), BF16)], place, masks[0], coupling[0], smem=2, plain=1
    )
    own_c = exchange(mine, None).reshape(n, n)
    own_g, own_s = green_local[:, 0], incident[:, 0].reshape(count, n, cols)

    size = lax.axis_size("slab")
    first_0, first_1 = call(first_kernel, [(vec, BF16), (vec, BF16)], own_g, own_s, flops=4 * unit)
    next_0 = lax.ppermute(first_0, "slab", [(i, i - 2) for i in range(2, size, 2)])
    next_1 = lax.ppermute(first_1, "slab", [(i, i - 1) for i in range(2, size, 2)])
    got_first = lax.ppermute(first_0, "slab", [(i + 1, i) for i in range(0, size, 2)])

    got_g = swap(call(split_kernel, [(mat, BF16)], which, own_g, smem=1))
    got_s = swap(call(split_kernel, [(vec, BF16)], which, own_s, smem=1))
    own_c, next_0, next_1, got_first, got_s = lax.optimization_barrier((own_c, next_0, next_1, got_first, got_s))
    got_c = swap(own_c)

    hops = lax.axis_size("slab") // 2 - 1
    green, source, c, ct, base, start, send = call(
        begin_kernel,
        [((2, *mat), BF16), ((2, *vec), BF16), (mat, BF16), (mat, BF16), (vec, F32), (vec, F32), (vec, BF16)],
        which, own_g, got_g, own_s, got_s, own_c, got_c, first_1, got_first, next_0, next_1,
        smem=1, far=4, scratch=[pltpu.SemaphoreType.DMA((4,))], flops=8 * unit,
    )
    flux = chip_hop(send, 1)
    step_a, through = call(
        compose_kernel, [(mat, BF16), (mat, BF16)], green, ct, scratch=[pltpu.VMEM(mat, BF16)], flops=16 * n**3
    )
    for _ in range(hops - 1):
        send = call(hop_kernel, [(vec, BF16)], through, start, flux, flops=2 * unit)
        flux = chip_hop(send, 1)
    back_a, back_b, back = call(compose_back_kernel, [(mat, BF16)] * 3, green, c, flops=16 * n**3)
    to_b, to_a, field_b, field_a = call(
        compose_turn_kernel,
        [(mat, BF16), (mat, BF16), (vec, F32), (vec, F32)],
        green, step_a, back_a, source, base, flops=16 * n**3 + 8 * unit,
    )
    start, end, send = call(
        turn_kernel, [(vec, F32), (vec, F32), (vec, BF16)], to_a, to_b, field_a, field_b, flux, flops=4 * unit
    )
    arrived = chip_hop(send, -1)
    for _ in range(hops - 1):
        send = call(hop_kernel, [(vec, BF16)], back, start, arrived, flops=2 * unit)
        arrived = chip_hop(send, -1)
    kept, send = call(
        finish_kernel, [(vec, BF16), (vec, BF16)], which, back, back_b, start, end, arrived, smem=1, flops=4 * unit
    )

    got = swap(send)
    weights = fermi(energy_index, 4.0 / (count * devices * modes))
    partial = call(
        density_kernel, [((nx, ny, nz * rows, 2 * n), BF16)], which, weights, kept, got, smem=2, flops=8 * unit
    )
    parts = exchange(partial, along_x)
    summed = jnp.sum(parts.astype(F32), axis=0).astype(BF16)
    parts = exchange(summed.reshape(ny * nz, rows, 2 * n), along_yz)
    density = jnp.sum(parts.astype(F32), axis=0).reshape(1, rows, 2, n)

    wave = ordered(core, kept, got)
    flow = pick(ct, core)
    outflow = jnp.stack([mul(flow, wave[e]) for e in range(count)]).astype(BF16)
    shape = (count, 1, n, 2, modes)
    return (wave.reshape(shape), outflow.reshape(shape), density)


def solution(mesh):
    return jax.shard_map(
        shards,
        mesh=mesh,
        in_specs=(
            P("energy", "slab", None, None, None),
            P("slab", "energy", None),
            P("slab", None, None),
            P("energy", "slab", None, None, None),
            P("energy"),
        ),
        out_specs=(
            P("energy", "slab", None, None, None),
            P("energy", "slab", None, None, None),
            P("slab", "energy", None, None),
        ),
        check_vma=False,
    )
```

```python
import jax
import jax.numpy as jnp
from jax import lax
from jax.experimental import pallas as pl
from jax.experimental.pallas import tpu as pltpu
from jax.sharding import PartitionSpec as P

BF16 = jnp.bfloat16
F32 = jnp.float32


def chip_hop(block, distance):
    size = lax.axis_size("slab")
    route = [(i, i + 2 * distance) for i in range(size) if 0 <= i + 2 * distance < size]
    return lax.ppermute(block, "slab", route)


def swap(block):
    route = [(i, i ^ 1) for i in range(lax.axis_size("slab"))]
    return lax.ppermute(block, "slab", route)


def pick(blocks, index):
    return lax.dynamic_index_in_dim(blocks, index, 0, keepdims=False)


def ordered(core, kept, got):
    even = core == 0
    return jnp.stack([jnp.where(even, kept, got), jnp.where(even, got, kept)])


def exchange(block, groups):
    return lax.all_to_all(block, "energy", 0, 0, axis_index_groups=groups, tiled=True)


def energy_grid(devices):
    return (2, 2, 2) if devices == 8 else (2, 4, devices // 8)


def mul(left, right):
    return lax.dot_general(left, right, (((1,), (0,)), ((), ())), preferred_element_type=F32)


def mul_transposed(left, right):
    return lax.dot_general(left, right, (((1,), (1,)), ((), ())), preferred_element_type=F32)


def turned(vector):
    k = vector.shape[1] // 2
    return jnp.concatenate([-vector[:, k:], vector[:, :k]], axis=1)


def apply(real, imag, vector):
    return mul(real, vector) + mul(imag, turned(vector))


def product(left, right, out):
    lr, li, rr, ri = left[0], left[1], right[0], right[1]
    out[0] = (mul(lr, rr) - mul(li, ri)).astype(BF16)
    out[1] = (mul(lr, ri) + mul(li, rr)).astype(BF16)


def rows_kernel(place, masks, rows, out):
    copies, count, n = out.shape
    blocks = masks.shape[1]
    tile = n // blocks
    here = (place[0] * count) // tile
    for j in range(blocks):
        at = slice(j * tile, (j + 1) * tile)
        present = masks[here, j].astype(F32)
        masked = (rows[:, at].astype(F32) * present).astype(BF16)
        for i in range(copies):
            out[i, :, at] = masked


def split_kernel(core, own, block):
    block[...] = own[1 - core[0]]


def first_kernel(g, src, here, there):
    here[...] = apply(g[0, 0], g[0, 1], src[0]).astype(BF16)
    there[...] = apply(g[1, 0], g[1, 1], src[1]).astype(BF16)


def begin_kernel(
    core, own_g, got_g, own_s, got_s, own_c, got_c, own_first, got_first, next_0, next_1,
    g, src, c, ct, base, start, send, sems,
):
    here = core[0]
    copies = [
        pltpu.make_async_copy(own_s.at[here], src.at[here], sems.at[0]),
        pltpu.make_async_copy(got_s, src.at[1 - here], sems.at[1]),
        pltpu.make_async_copy(own_g.at[here], g.at[here], sems.at[2]),
        pltpu.make_async_copy(got_g, g.at[1 - here], sems.at[3]),
    ]
    for copy in copies:
        copy.start()
    c[here] = own_c[...]
    c[1 - here] = got_c[...]
    ct[0] = c[0].T
    ct[1] = c[1].T
    first = jnp.where(here == 0, got_first[...], own_first[...])
    following = next_0[...] + next_1[...]
    copies[0].wait()
    copies[1].wait()
    base_a = src[0].astype(F32) + mul(c[0], first)
    base[...] = base_a
    copies[2].wait()
    copies[3].wait()
    field = apply(g[0, 0], g[0, 1], base_a.astype(BF16)).astype(BF16)
    summed = src[1].astype(F32) + mul(c[1], following) + mul(ct[0], field)
    field = apply(g[1, 0], g[1, 1], summed.astype(BF16)).astype(BF16)
    flux = mul(ct[1], field)
    start[...] = flux
    send[...] = flux.astype(BF16)


def compose_kernel(g, ct, step_a, through, step_b):
    step_a[0] = mul(ct[0], g[0, 0]).astype(BF16)
    step_a[1] = mul(ct[0], g[0, 1]).astype(BF16)
    step_b[0] = mul(ct[1], g[1, 0]).astype(BF16)
    step_b[1] = mul(ct[1], g[1, 1]).astype(BF16)
    product(step_b, step_a, through)


def compose_back_kernel(g, c, step_a, src, base, back_a, back_b, back, to_b, field_b):
    back_a[0] = mul(g[0, 0], c[0]).astype(BF16)
    back_a[1] = mul(g[0, 1], c[0]).astype(BF16)
    back_b[0] = mul(g[1, 0], c[1]).astype(BF16)
    back_b[1] = mul(g[1, 1], c[1]).astype(BF16)
    product(back_a, back_b, back)
    gbr, gbi = g[1, 0], g[1, 1]
    sr, si = step_a[0], step_a[1]
    to_b[0] = (mul(gbr, sr) - mul(gbi, si)).astype(BF16)
    to_b[1] = (mul(gbr, si) + mul(gbi, sr)).astype(BF16)
    flux_a = apply(sr, si, base[...].astype(BF16))
    field_b[...] = apply(gbr, gbi, (src[1].astype(F32) + flux_a).astype(BF16))


def compose_turn_a_kernel(g, back_a, src, to_b, field_b, to_a, field_a):
    ar, ai = back_a[0], back_a[1]
    br, bi = to_b[0], to_b[1]
    to_a[0] = (g[0, 0].astype(F32) + mul(ar, br) - mul(ai, bi)).astype(BF16)
    to_a[1] = (g[0, 1].astype(F32) + mul(ar, bi) + mul(ai, br)).astype(BF16)
    field_a[...] = apply(g[0, 0], g[0, 1], src[0]) + apply(ar, ai, field_b[...].astype(BF16))


def hop_kernel(matrix, start, arrived, send):
    send[...] = (start[...] + apply(matrix[0], matrix[1], arrived[...])).astype(BF16)


def turn_kernel(to_a, to_b, field_a, field_b, flux, start, end, send):
    arrived = flux[...]
    wave = field_a[...] + apply(to_a[0], to_a[1], arrived)
    start[...] = wave
    send[...] = wave.astype(BF16)
    end[...] = field_b[...] + apply(to_b[0], to_b[1], arrived)


def finish_kernel(core, back, back_b, start, end, arrived, keep, send):
    wave_a = (start[...] + apply(back[0], back[1], arrived[...])).astype(BF16)
    wave_b = (end[...] + apply(back_b[0], back_b[1], arrived[...])).astype(BF16)

    @pl.when(core[0] == 0)
    def _():
        keep[...] = wave_a
        send[...] = wave_b

    @pl.when(core[0] != 0)
    def _():
        keep[...] = wave_b
        send[...] = wave_a


def density_kernel(place, weights, kept, got, out):
    n = kept.shape[0]
    ny, rows, _ = out.shape
    here = weights[place[0]]
    there = weights[1 - place[0]]
    for y in range(ny):
        at = pl.multiple_of(y * (n // ny) + place[1] * rows, rows)
        real = jnp.zeros((rows, n), F32)
        imag = jnp.zeros((rows, n), F32)
        for weight, wave in ((here, kept), (there, got)):
            w = wave[...]
            scaled = (wave[pl.ds(at, rows), :].astype(F32) * weight).astype(BF16)
            real = real + mul_transposed(scaled, w)
            imag = imag + mul_transposed(scaled, turned(w))
        out[y, :, :n] = real.astype(out.dtype)
        out[y, :, n:] = imag.astype(out.dtype)


def sum_kernel(own, *refs):
    *others, out = refs
    total = own[...]
    for other in others:
        total = total + other[...].astype(F32)
    out[...] = total.astype(BF16)


def call(kernel, out_shapes, *operands, scratch=(), flops=0, smem=0, far=0, plain=0):
    whole = pl.BlockSpec(memory_space=pltpu.VMEM)
    specs = [pl.BlockSpec(memory_space=pltpu.SMEM)] * smem + [pl.BlockSpec(memory_space=pltpu.HBM)] * far
    outs = [pltpu.VMEM(s, d) if i >= plain else jax.ShapeDtypeStruct(s, d) for i, (s, d) in enumerate(out_shapes)]
    first = smem + far
    space = lambda i: pltpu.HBM if i < first else pltpu.VMEM
    operands = [
        o if i < smem else pltpu.with_memory_space_constraint(o, space(i)) for i, o in enumerate(operands)
    ]
    result = pl.pallas_call(
        kernel,
        out_shape=outs,
        in_specs=specs + [whole] * (len(operands) - first),
        out_specs=[whole] * len(outs),
        scratch_shapes=list(scratch),
        cost_estimate=pl.CostEstimate(flops=flops, transcendentals=0, bytes_accessed=1 << 20),
        compiler_params=pltpu.CompilerParams(vmem_limit_bytes=24 << 20),
    )(*operands)
    return result if len(outs) > 1 else result[0]


def fermi(index_values, scale):
    exponent = (index_values.astype(F32) - 128.0) / 24.0
    return scale / (1.0 + jnp.exp(exponent))


def shards(green_local, coupling, masks, incident, energy_index):
    count = green_local.shape[0]
    n = green_local.shape[3]
    modes = incident.shape[4]
    cols = 2 * modes
    devices = lax.axis_size("energy")
    ny, nx, nz = energy_grid(devices)
    at = lambda y, x, z: (y * nx + x) * nz + z
    along_yz = [[at(y, x, z) for y in range(ny) for z in range(nz)] for x in range(nx)]
    rows = coupling.shape[1]
    tile = n // masks.shape[1]
    vec = (n, cols)
    mat = (2, n, n)
    unit = 2 * n * n * cols

    core = lax.rem(lax.axis_index("slab"), 2)
    which = core.reshape(1)

    place = lax.axis_index("energy").reshape(1)
    mine = call(
        rows_kernel, [((devices, rows, n), BF16)], place, masks[0], coupling[0], smem=2, plain=1
    )
    own_c = exchange(mine, None).reshape(n, n)
    own_g, own_s = green_local[:, 0], incident[:, 0].reshape(count, n, cols)

    size = lax.axis_size("slab")
    first_0, first_1 = call(first_kernel, [(vec, BF16), (vec, BF16)], own_g, own_s, flops=4 * unit)
    next_0 = lax.ppermute(first_0, "slab", [(i, i - 2) for i in range(2, size, 2)])
    next_1 = lax.ppermute(first_1, "slab", [(i, i - 1) for i in range(2, size, 2)])
    got_first = lax.ppermute(first_0, "slab", [(i + 1, i) for i in range(0, size, 2)])

    got_g = swap(call(split_kernel, [(mat, BF16)], which, own_g, smem=1))
    got_s = swap(call(split_kernel, [(vec, BF16)], which, own_s, smem=1))
    own_c, next_0, next_1, got_first, got_s = lax.optimization_barrier((own_c, next_0, next_1, got_first, got_s))
    got_c = swap(own_c)

    hops = lax.axis_size("slab") // 2 - 1
    green, source, c, ct, base, start, send = call(
        begin_kernel,
        [((2, *mat), BF16), ((2, *vec), BF16), (mat, BF16), (mat, BF16), (vec, F32), (vec, F32), (vec, BF16)],
        which, own_g, got_g, own_s, got_s, own_c, got_c, first_1, got_first, next_0, next_1,
        smem=1, far=4, scratch=[pltpu.SemaphoreType.DMA((4,))], flops=8 * unit,
    )
    flux = chip_hop(send, 1)
    step_a, through = call(
        compose_kernel, [(mat, BF16), (mat, BF16)], green, ct, scratch=[pltpu.VMEM(mat, BF16)], flops=16 * n**3
    )
    for step in range(hops - 1):
        if step == hops - 2:
            back_a, back_b, back, to_b, field_b = call(
                compose_back_kernel,
                [(mat, BF16)] * 4 + [(vec, F32)],
                green, c, step_a, source, base, flops=24 * n**3 + 4 * unit,
            )
            flux, back_a, to_b = lax.optimization_barrier((flux, back_a, to_b))
        send = call(hop_kernel, [(vec, BF16)], through, start, flux, flops=2 * unit)
        flux = chip_hop(send, 1)
    to_a, field_a = call(
        compose_turn_a_kernel,
        [(mat, BF16), (vec, F32)],
        green, back_a, source, to_b, field_b, flops=8 * n**3 + 4 * unit,
    )
    start, end, send = call(
        turn_kernel, [(vec, F32), (vec, F32), (vec, BF16)], to_a, to_b, field_a, field_b, flux, flops=4 * unit
    )
    arrived = chip_hop(send, -1)
    for _ in range(hops - 1):
        send = call(hop_kernel, [(vec, BF16)], back, start, arrived, flops=2 * unit)
        arrived = chip_hop(send, -1)
    kept, send = call(
        finish_kernel, [(vec, BF16), (vec, BF16)], which, back, back_b, start, end, arrived, smem=1, flops=4 * unit
    )

    got = swap(send)
    weights = fermi(energy_index, 4.0 / (count * devices * modes))
    x_here = lax.rem(lax.axis_index("energy") // nz, nx)
    block = (ny, nz * rows, 2 * n)

    def density_of(step, kind):
        place = jnp.stack([core, lax.rem(x_here + step, nx)])
        return call(density_kernel, [(block, kind)], place, weights, kept, got, smem=2, flops=2 * unit)

    arrived = []
    for step in (nx // 2, *[k for k in range(1, nx) if k != nx // 2]):
        route = [
            (at(y, x, z), at(y, (x + step) % nx, z)) for y in range(ny) for x in range(nx) for z in range(nz)
        ]
        arrived.append(lax.ppermute(density_of(step, BF16), "energy", route))
    summed = call(sum_kernel, [(block, BF16)], density_of(0, F32), *arrived)
    parts = exchange(summed.reshape(ny * nz, rows, 2 * n), along_yz)
    density = jnp.sum(parts.astype(F32), axis=0).reshape(1, rows, 2, n)

    wave = ordered(core, kept, got)
    flow = pick(ct, core)
    outflow = jnp.stack([mul(flow, wave[e]) for e in range(count)]).astype(BF16)
    shape = (count, 1, n, 2, modes)
    return (wave.reshape(shape), outflow.reshape(shape), density)


def solution(mesh):
    return jax.shard_map(
        shards,
        mesh=mesh,
        in_specs=(
            P("energy", "slab", None, None, None),
            P("slab", "energy", None),
            P("slab", None, None),
            P("energy", "slab", None, None, None),
            P("energy"),
        ),
        out_specs=(
            P("energy", "slab", None, None, None),
            P("energy", "slab", None, None, None),
            P("slab", "energy", None, None),
        ),
        check_vma=False,
    )
```
